128 devices in a mesh: slab: 4 (over x), row: 2 (over core), col: 16 (over z, y).
Axes of the slice: x: 4, y: 4, z: 4, core: 2. Of those that a mesh axis runs over, the one named last changes fastest.
Arguments:
- sources: float32 [4, 16, 2, 384, 256], P('slab', 'col', 'row'), may hold values from -6 to 6
- tr_vals: float32 [4, 16, 2, 6, 12, 128, 128], P('slab', 'col', 'row'), may hold values from -0.09375 to 0.09375
- tr_cols: int32 [4, 16, 2, 6, 12], P('slab', 'col', 'row'), may hold values from 0 to 47, as said below
- rf_vals: float32 [4, 16, 2, 6, 12, 128, 128], P('slab', 'col', 'row'), may hold values from -0.078125 to 0.078125
- rf_cols: int32 [4, 16, 2, 6, 12], P('slab', 'col', 'row'), may hold values from 0 to 47, as said below
Outputs:
- total_traces: float32 [4, 16, 2, 384, 256], P('slab', 'col', 'row')
The draws below stay inside these ranges and needn't reach their ends.
Inputs may be any that keep to these rules, and one draw needn't show every extreme that they name: `tr_cols`: each block row lists 12 different column blocks of its column group. `rf_cols`: each block row lists 12 different column blocks of its column group.
All inputs are finite; a program needn't handle non-finite values.
Results may differ from the reference program's by a relative error of at most 0.0001.
Values sent between devices are 32-bit elements; how exact they have to be, the bound alone decides.
A program may use at most 128 MiB of HBM per device.

```python
import jax
import jax.numpy as jnp
from jax import lax

M = 12288
BS = 128
S = 256
SLABS = 4
GC = 16
GR = 2
P_SIZE = 384
RB = 6
CB = 48
K = 12


def pick_blocks(key):
    scores = jax.random.randint(key, (SLABS, GC, GR, RB, CB), 0, 1 << 20, dtype=jnp.int32)
    scores = scores * CB + jnp.arange(CB, dtype=jnp.int32)
    order = jnp.argsort(scores, axis=-1)[..., :K]
    return order.astype(jnp.int32)


def draw_tr_cols(key, part):
    return pick_blocks(jax.random.fold_in(key, 11))


def draw_rf_cols(key, part):
    return pick_blocks(jax.random.fold_in(key, 23))


def levels(rng, shape, split, smallest, largest):
    factor_of, own = 1.0, jax.random.fold_in(rng, 6)
    for axis_at, parts in split:
        steps = jnp.exp(jax.random.uniform(jax.random.fold_in(own, axis_at), (parts,), jnp.float32, smallest / len(split), largest / len(split)))
        factor_of = factor_of * jnp.repeat(steps, shape[axis_at] // parts).reshape([-1 if axis == axis_at else 1 for axis in range(len(shape))])
    return factor_of


def bell_draw(key, dims, spread, reach, shards=(), kind=jnp.bfloat16):
    level = levels(key, dims, shards, -0.22, 0.18) if shards else 1.0
    entries = jax.random.normal(key, dims, jnp.float32) * spread * level
    return jnp.minimum(jnp.maximum(entries, -reach), reach).astype(kind)


def setup_inputs(seed: int = 0) -> dict:
    key_of = jax.random.split(jax.random.key(seed), 6)
    return {
        "sources": bell_draw(key_of[0], (SLABS, GC, GR, P_SIZE, S), 1.0, 6.0, ((0, 4), (1, 16), (2, 2)), jnp.float32),
        "tr_vals": bell_draw(key_of[1], (SLABS, GC, GR, RB, K, BS, BS), (M // 3) ** -0.5, 0.09375, ((0, 4), (1, 16), (2, 2)), jnp.float32),
        "tr_cols": draw_tr_cols(jax.random.fold_in(key_of[5], 71), 0),
        "rf_vals": bell_draw(key_of[3], (SLABS, GC, GR, RB, K, BS, BS), (M // 2) ** -0.5, 0.078125, ((0, 4), (1, 16), (2, 2)), jnp.float32),
        "rf_cols": draw_rf_cols(jax.random.fold_in(key_of[5], 71), 0),
    }


def apply_operator(values, columns, trace):
    groups_c = columns.shape[0]
    groups_r = columns.shape[1]
    width_cols = trace.shape[3]
    tiles = jnp.transpose(trace, (1, 0, 2, 3)).reshape(groups_r, -1, BS, width_cols)
    which_r = jnp.arange(groups_r, dtype=jnp.int32)[None, :, None, None]
    picked = tiles[which_r, columns]
    summed = jnp.einsum("crikab,crikbs->cias", values, picked, precision=lax.Precision.HIGHEST)
    return summed.reshape(groups_c, groups_r, -1, width_cols)


def reference(sources, tr_vals, tr_cols, rf_vals, rf_cols):
    down_list = []
    refl_list = []
    previous = jnp.zeros(sources.shape[1:], jnp.float32)
    for section in range(SLABS):
        incident = sources[section] + previous
        moved = apply_operator(tr_vals[section], tr_cols[section], incident)
        reflected = apply_operator(rf_vals[section], rf_cols[section], incident)
        down_list.append(moved)
        refl_list.append(reflected)
        previous = moved
    up_list = [None] * SLABS
    above = jnp.zeros(sources.shape[1:], jnp.float32)
    for section in range(SLABS - 1, -1, -1):
        above = apply_operator(tr_vals[section], tr_cols[section], refl_list[section] + above)
        up_list[section] = above
    return jnp.stack(down_list) + jnp.stack(up_list)
```

```python
import functools

import jax
import jax.numpy as jnp
from jax import lax
from jax.experimental import pallas as pl
from jax.experimental.pallas import tpu as pltpu
from jax.sharding import PartitionSpec as P

MESH = pl.DeviceIdType.MESH
BATCHES = 8
STAGE = 5
TURN = 5
RING = 4
PIECES = RING * RING
BLOCK = 128


def kernel(
    dims,
    src_ref,
    trv_ref,
    rfv_ref,
    trc_ref,
    rfc_ref,
    out_ref,
    gat,
    xs,
    wts,
    stage,
    src_t,
    xrecv,
    down_s,
    refl_s,
    up_s,
    own,
    ex_src,
    ex_dst,
    cols,
    load_sem,
    tree_recv,
    tree_send,
    ex_recv,
    ex_send,
    x_recv,
    x_send,
):
    batches, width, blocks, row_blocks, picks, slabs = dims
    rows = blocks * width
    half = rows // 2
    own_rows = row_blocks // 2
    s = lax.axis_index("slab")
    r = lax.axis_index("row")
    c = lax.axis_index("col")
    y = lax.rem(c, RING)
    z = lax.div(c, RING)
    a = y * (1 - r) + z * r
    b = z * (1 - r) + y * r
    step_a = 1 + (RING - 1) * r
    step_b = RING - (RING - 1) * r

    def col(da, db):
        return lax.rem(a + da + RING, RING) * step_a + lax.rem(b + db + RING, RING) * step_b

    def plane(da, db):
        return (s, r, col(da, db))

    partner = (s, 1 - r, c)
    below = (lax.rem(s + 1, slabs), r, c)
    above = (lax.rem(s + slabs - 1, slabs), r, c)

    def load(op, i):
        ref = trv_ref if op == 0 else rfv_ref
        return pltpu.make_async_copy(ref.at[i], stage.at[op * row_blocks + i], load_sem.at[op * row_blocks + i])

    for op in range(2):
        for i in range(row_blocks):
            load(op, i).start()

    barrier = pltpu.get_barrier_semaphore()
    greeted = (plane(1, 0), plane(-1, 0), plane(0, 1), plane(0, -1), partner, below, above)
    for device in greeted:
        pl.semaphore_signal(barrier, inc=1, device_id=device, device_id_type=MESH)

    for i in range(row_blocks):
        for k in range(picks):
            cols[0, i, k] = trc_ref[i, k]
            cols[1, i, k] = rfc_ref[i, k]
    for j in range(blocks):
        turned = jnp.transpose(src_ref[j * BLOCK : (j + 1) * BLOCK, :])
        for n in range(batches):
            src_t[n, j * width : (j + 1) * width, :] = turned[n * width : (n + 1) * width, :]

    pl.semaphore_wait(barrier, len(greeted))

    def tree(n, piece, part, device, group):
        where = gat.at[n, piece] if part is None else gat.at[n, piece, pl.ds(part * half, half)]
        pltpu.make_async_remote_copy(
            src_ref=where,
            dst_ref=where,
            send_sem=tree_send.at[n],
            recv_sem=tree_recv.at[n, group],
            device_id=device,
            device_id_type=MESH,
        ).start()

    def tree_wait(n, group, count):
        some = gat.at[n, pl.ds(0, count)]
        pltpu.make_async_copy(some, some, tree_recv.at[n, group]).wait()

    def both_sides(n, piece, group):
        tree(n, piece, None, plane(0, 1), group)
        tree(n, piece, None, plane(0, -1), group)

    def halves(n, da):
        tree(n, col(da, -1), 0, plane(0, 1), 5)
        tree(n, col(da, 1), 1, plane(0, -1), 5)

    def x_copy(source, n, device):
        return pltpu.make_async_remote_copy(
            src_ref=source,
            dst_ref=xrecv.at[n],
            send_sem=x_send.at[n],
            recv_sem=x_recv.at[n],
            device_id=device,
            device_id_type=MESH,
        )

    def inject(n, batch, is_down):
        @pl.when(is_down & (s == 0))
        def _():
            gat[n, c] = src_t[batch]

        @pl.when(jnp.logical_not(is_down) & (s == slabs - 1))
        def _():
            gat[n, c] = refl_s[batch]

        @pl.when(is_down & (s > 0))
        def _():
            x_copy(xrecv.at[n], n, above).wait_recv()
            gat[n, c] = src_t[batch] + xrecv[n]

        @pl.when(jnp.logical_not(is_down) & (s < slabs - 1))
        def _():
            x_copy(xrecv.at[n], n, above).wait_recv()
            gat[n, c] = refl_s[batch] + xrecv[n]

        tree(n, c, None, plane(1, 0), 0)
        tree(n, c, None, plane(-1, 0), 0)
        both_sides(n, c, 2)

    def relay_1(n, batch, is_down):
        tree_wait(n, 0, 2)
        tree(n, col(-1, 0), 0, plane(1, 0), 1)
        tree(n, col(1, 0), 1, plane(-1, 0), 1)
        both_sides(n, col(-1, 0), 3)
        both_sides(n, col(1, 0), 3)
        tree_wait(n, 2, 2)
        halves(n, 0)

    def relay_2(n, batch, is_down):
        tree_wait(n, 1, 1)
        both_sides(n, col(2, 0), 4)
        tree_wait(n, 3, 4)
        halves(n, -1)
        halves(n, 1)

    def relay_3(n, batch, is_down):
        tree_wait(n, 4, 2)
        halves(n, 2)

    def prepare(item, carry):
        pltpu.make_async_copy(trv_ref.at[0], stage.at[item], load_sem.at[item]).wait()
        for k in range(picks):
            value = stage[item, k]
            high = value.astype(jnp.bfloat16)
            low = (value - high.astype(jnp.float32)).astype(jnp.bfloat16)
            wts[item, 0:BLOCK, k * BLOCK : (k + 1) * BLOCK] = high
            wts[item, BLOCK : 2 * BLOCK, k * BLOCK : (k + 1) * BLOCK] = low
        return carry

    def ex_copy(n, op):
        return pltpu.make_async_remote_copy(
            src_ref=ex_src.at[n, op],
            dst_ref=ex_dst.at[n, op],
            send_sem=ex_send.at[n, op],
            recv_sem=ex_recv.at[n, op],
            device_id=partner,
            device_id_type=MESH,
        )

    def product(op, i):
        picked = jnp.concatenate([xs[cols[op, i, k]] for k in range(picks)], axis=1)
        full = lax.dot_general(
            picked,
            wts[op * row_blocks + i],
            (((1,), (1,)), ((), ())),
            preferred_element_type=jnp.float32,
        )
        high, low = full[:width], full[width:]
        return high[:, :BLOCK] + ((high[:, BLOCK:] + low[:, :BLOCK]) + low[:, BLOCK:])

    def apply(n, op):
        for j in range(own_rows):
            ex_src[n, op, j * width : (j + 1) * width, :] = product(op, (1 - r) * own_rows + j)
        ex_copy(n, op).start()
        for j in range(own_rows):
            own[op, j * width : (j + 1) * width, :] = product(op, r * own_rows + j)

    def finish(n, batch, is_down):
        tree_wait(n, 5, RING)
        for p in range(PIECES):
            for j in range(blocks):
                value = gat[n, p, j * width : (j + 1) * width, :]
                high = value.astype(jnp.bfloat16)
                xs[p * blocks + j, 0:width, :] = high
                xs[p * blocks + j, width : 2 * width, :] = (value - high.astype(jnp.float32)).astype(jnp.bfloat16)
        apply(n, 0)

        @pl.when(is_down)
        def _():
            apply(n, 1)
            ex_copy(n, 0).wait_recv()
            down_s[batch] = own[0] + ex_dst[n, 0]

            @pl.when(s < slabs - 1)
            def _():
                x_copy(down_s.at[batch], n, below).start()

            ex_copy(n, 1).wait_recv()
            refl_s[batch] = own[1] + ex_dst[n, 1]

        @pl.when(jnp.logical_not(is_down))
        def _():
            ex_copy(n, 0).wait_recv()
            up_s[batch] = own[0] + ex_dst[n, 0]

            @pl.when(s > 0)
            def _():
                x_copy(up_s.at[batch], n, above).start()

            out_ref[batch] = down_s[batch] + up_s[batch]

    offset = (2 * (slabs - 1) - 2 * s) * STAGE + TURN

    def phase(body, slot, delay, first=0):
        at = slot - delay + 2 * batches
        is_down = lax.rem(at, 2) == 0
        batch = jnp.where(is_down, lax.div(at, 2) - batches, lax.div(at - offset + 64, 2) - batches - 32)
        valid = (batch >= 0) & (batch < batches)

        @pl.when(valid)
        def _():
            body(jnp.where(is_down, batch, batches + batch), batch, is_down)

    items = 2 * row_blocks
    each = 3

    @pl.when(s > 0)
    def _():
        lax.fori_loop(0, items, prepare, 0)

    def slot_body(slot, carry):
        phase(relay_3, slot, 3)
        phase(relay_2, slot, 2)
        phase(relay_1, slot, 1)
        phase(inject, slot, 0)

        @pl.when((s == 0) & (slot < items // each))
        def _():
            lax.fori_loop(slot * each, slot * each + each, prepare, 0)

        phase(finish, slot, 4)
        return carry

    lax.fori_loop(0, 2 * (batches - 1) + offset + 5, slot_body, 0)

    def drain(n, carry):
        sent = gat.at[n, pl.ds(0, PIECES - 1)]
        pltpu.make_async_copy(sent, sent, tree_send.at[n]).wait()
        ex_copy(n, 0).wait_send()

        @pl.when(n < batches)
        def _():
            ex_copy(n, 1).wait_send()

        @pl.when(((n < batches) & (s < slabs - 1)) | ((n >= batches) & (s > 0)))
        def _():
            x_copy(up_s.at[0], n, above).wait_send()

        return carry

    lax.fori_loop(0, 2 * batches, drain, 0)


def shards(slabs, sources, tr_vals, tr_cols, rf_vals, rf_cols):
    source = sources[0, 0, 0]
    rows_in, span = source.shape
    row_blocks, picks = tr_cols.shape[-2:]
    blocks = rows_in // BLOCK
    batches = BATCHES
    width = span // batches
    rows = blocks * width
    tasks = 2 * batches
    f32, bf16 = jnp.float32, jnp.bfloat16
    vmem = pl.BlockSpec(memory_space=pltpu.VMEM)
    smem = pl.BlockSpec(memory_space=pltpu.SMEM)
    hbm = pl.BlockSpec(memory_space=pl.ANY)
    dma = pltpu.SemaphoreType.DMA
    out = pl.pallas_call(
        functools.partial(kernel, (batches, width, blocks, row_blocks, picks, slabs)),
        out_shape=jax.ShapeDtypeStruct((batches, rows, BLOCK), f32),
        in_specs=[vmem, hbm, hbm, smem, smem],
        out_specs=vmem,
        scratch_shapes=[
            pltpu.VMEM((tasks, PIECES, rows, BLOCK), f32),
            pltpu.VMEM((PIECES * blocks, 2 * width, BLOCK), bf16),
            pltpu.VMEM((2 * row_blocks, 2 * BLOCK, picks * BLOCK), bf16),
            pltpu.VMEM((2 * row_blocks, picks, BLOCK, BLOCK), f32),
            pltpu.VMEM((batches, rows, BLOCK), f32),
            pltpu.VMEM((tasks, rows, BLOCK), f32),
            pltpu.VMEM((batches, rows, BLOCK), f32),
            pltpu.VMEM((batches, rows, BLOCK), f32),
            pltpu.VMEM((batches, rows, BLOCK), f32),
            pltpu.VMEM((2, rows, BLOCK), f32),
            pltpu.VMEM((tasks, 2, rows, BLOCK), f32),
            pltpu.VMEM((tasks, 2, rows, BLOCK), f32),
            pltpu.SMEM((2, row_blocks, picks), jnp.int32),
            dma((2 * row_blocks,)),
            dma((tasks, 6)),
            dma((tasks,)),
            dma((tasks, 2)),
            dma((tasks, 2)),
            dma((tasks,)),
            dma((tasks,)),
        ],
        compiler_params=pltpu.CompilerParams(
            collective_id=0,
            has_side_effects=True,
            vmem_limit_bytes=60 * 1024 * 1024,
        ),
    )(source, tr_vals[0, 0, 0], rf_vals[0, 0, 0], tr_cols[0, 0, 0], rf_cols[0, 0, 0])
    out = out.reshape(batches, blocks, width, BLOCK).transpose(1, 3, 0, 2)
    return out.reshape(rows_in, span)[None, None, None]


def solution(mesh):
    placed = (
        P("slab", "col", "row", None, None),
        P("slab", "col", "row", None, None, None, None),
        P("slab", "col", "row", None, None),
        P("slab", "col", "row", None, None, None, None),
        P("slab", "col", "row", None, None),
    )
    return jax.shard_map(
        functools.partial(shards, mesh.shape["slab"]),
        mesh=mesh,
        in_specs=placed,
        out_specs=P("slab", "col", "row", None, None),
        check_vma=False,
    )
```

```python
import functools

import jax
import jax.numpy as jnp
from jax import lax
from jax.experimental import pallas as pl
from jax.experimental.pallas import tpu as pltpu
from jax.sharding import PartitionSpec as P

MESH = pl.DeviceIdType.MESH
BATCHES = 8
RING = 4
PIECES = RING * RING
BLOCK = 128
SPREAD = 1
DONE = 2
TURN = 2
GAP = 5
ROUND = (
    ("spread", "down", SPREAD),
    ("spread", "up", SPREAD),
    ("inject", "down", 0),
    ("prepare", "", 0),
    ("finish", "down", DONE),
    ("inject", "up", 0),
    ("finish", "up", DONE),
)


def kernel(
    dims,
    src_ref,
    trv_ref,
    rfv_ref,
    trc_ref,
    rfc_ref,
    out_ref,
    gat,
    xs,
    wts,
    stage,
    src_t,
    xrecv,
    down_s,
    refl_s,
    up_s,
    own,
    ex_src,
    ex_dst,
    cols,
    load_sem,
    first_recv,
    second_recv,
    tree_send,
    ex_recv,
    ex_send,
    x_recv,
    x_send,
):
    batches, width, blocks, row_blocks, picks, slabs = dims
    rows = blocks * width
    half = rows // 2
    own_rows = row_blocks // 2
    s = lax.axis_index("slab")
    r = lax.axis_index("row")
    c = lax.axis_index("col")
    y = lax.rem(c, RING)
    z = lax.div(c, RING)
    a = y * (1 - r) + z * r
    b = z * (1 - r) + y * r
    step_a = 1 + (RING - 1) * r
    step_b = RING - (RING - 1) * r

    def col(da, db):
        return lax.rem(a + da + RING, RING) * step_a + lax.rem(b + db + RING, RING) * step_b

    def plane(da, db):
        return (s, r, col(da, db))

    partner = (s, 1 - r, c)
    below = (lax.rem(s + 1, slabs), r, c)
    above = (lax.rem(s + slabs - 1, slabs), r, c)

    def load(op, i):
        ref = trv_ref if op == 0 else rfv_ref
        return pltpu.make_async_copy(ref.at[i], stage.at[op * row_blocks + i], load_sem.at[op * row_blocks + i])

    for op in range(2):
        for i in range(row_blocks):
            load(op, i).start()

    barrier = pltpu.get_barrier_semaphore()
    near = [plane(d, 0) for d in (1, 2, -1)] + [plane(0, d) for d in (1, 2, -1)]
    greeted = (*near, partner, below, above)
    for device in greeted:
        pl.semaphore_signal(barrier, inc=1, device_id=device, device_id_type=MESH)

    def place(column):
        piece = lax.div(column, blocks)
        turned = lax.rem(piece, RING) * RING + lax.div(piece, RING)
        return jnp.where(r == 0, piece, turned) * blocks + lax.rem(column, blocks)

    for i in range(row_blocks):
        for k in range(picks):
            cols[0, i, k] = place(trc_ref[i, k])
            cols[1, i, k] = place(rfc_ref[i, k])
    for j in range(blocks):
        turned = jnp.transpose(src_ref[j * BLOCK : (j + 1) * BLOCK, :])
        for n in range(batches):
            src_t[n, j * width : (j + 1) * width, :] = turned[n * width : (n + 1) * width, :]

    pl.semaphore_wait(barrier, len(greeted))

    mine = b * RING + a

    def tree(where, n, device, arrival):
        pltpu.make_async_remote_copy(
            src_ref=where,
            dst_ref=where,
            send_sem=tree_send.at[n],
            recv_sem=arrival,
            device_id=device,
            device_id_type=MESH,
        ).start()

    def arrived(n, count, semaphore):
        some = gat.at[n, pl.ds(0, count)]
        pltpu.make_async_copy(some, some, semaphore).wait()

    def split(n, slot, group):
        for p in range(RING):
            at = group * RING + p
            for j in range(blocks):
                value = gat[n, at, j * width : (j + 1) * width, :]
                high = value.astype(jnp.bfloat16)
                xs[slot, at * blocks + j, 0:width, :] = high
                xs[slot, at * blocks + j, width : 2 * width, :] = (value - high.astype(jnp.float32)).astype(jnp.bfloat16)

    def x_copy(source, n, device):
        return pltpu.make_async_remote_copy(
            src_ref=source,
            dst_ref=xrecv.at[n],
            send_sem=x_send.at[n],
            recv_sem=x_recv.at[n],
            device_id=device,
            device_id_type=MESH,
        )

    def inject(n, batch, slot, is_down):
        held = src_t if is_down else refl_s
        end = 0 if is_down else slabs - 1

        @pl.when(s == end)
        def _():
            gat[n, mine] = held[batch]

        @pl.when(s != end)
        def _():
            x_copy(xrecv.at[n], n, above).wait_recv()
            gat[n, mine] = held[batch] + xrecv[n]

        for da in (2, 1, -1):
            tree(gat.at[n, mine], n, plane(da, 0), first_recv.at[n])

    def spread(n, batch, slot, is_down):
        arrived(n, RING - 1, first_recv.at[n])
        for order, db in enumerate((2, 1, -1)):
            tree(gat.at[n, pl.ds(b * RING, RING)], n, plane(0, db), second_recv.at[n, order])
        split(n, slot, b)

    def prepare(item, carry):
        pltpu.make_async_copy(trv_ref.at[0], stage.at[item], load_sem.at[item]).wait()
        for k in range(picks):
            value = stage[item, k]
            high = value.astype(jnp.bfloat16)
            low = (value - high.astype(jnp.float32)).astype(jnp.bfloat16)
            wts[item, 0:BLOCK, k * BLOCK : (k + 1) * BLOCK] = high
            wts[item, BLOCK : 2 * BLOCK, k * BLOCK : (k + 1) * BLOCK] = low
        return carry

    def ex_copy(n, op):
        return pltpu.make_async_remote_copy(
            src_ref=ex_src.at[n, op],
            dst_ref=ex_dst.at[n, op],
            send_sem=ex_send.at[n, op],
            recv_sem=ex_recv.at[n, op],
            device_id=partner,
            device_id_type=MESH,
        )

    def product(slot, op, i):
        picked = jnp.concatenate([xs[slot, cols[op, i, k]] for k in range(picks)], axis=1)
        full = lax.dot_general(
            picked,
            wts[op * row_blocks + i],
            (((1,), (1,)), ((), ())),
            preferred_element_type=jnp.float32,
        )
        high, low = full[:width], full[width:]
        return high[:, :BLOCK] + ((high[:, BLOCK:] + low[:, :BLOCK]) + low[:, BLOCK:])

    def partner_rows(n, slot, op):
        for j in range(own_rows):
            ex_src[n, op, j * width : (j + 1) * width, :] = product(slot, op, (1 - r) * own_rows + j)
        ex_copy(n, op).start()

    def my_rows(n, slot, op):
        for j in range(own_rows):
            own[op, j * width : (j + 1) * width, :] = product(slot, op, r * own_rows + j)

    def total(n, op):
        ex_copy(n, op).wait_recv()
        return own[op] + ex_dst[n, op]

    def finish(n, batch, slot, is_down):
        for order, db in ((1, 1), (2, -1), (0, 2)):
            arrived(n, RING, second_recv.at[n, order])
            split(n, slot, lax.rem(b - db + RING, RING))
        if is_down:
            first = lax.div(s, slabs - 1)
            second = 1 - first
            partner_rows(n, slot, first)
            my_rows(n, slot, first)
            partner_rows(n, slot, second)

            @pl.when(s < slabs - 1)
            def _():
                down_s[batch] = total(n, 0)
                x_copy(down_s.at[batch], n, below).start()

            @pl.when(s == slabs - 1)
            def _():
                refl_s[batch] = total(n, 1)

            my_rows(n, slot, second)

            @pl.when(s < slabs - 1)
            def _():
                refl_s[batch] = total(n, 1)

            @pl.when(s == slabs - 1)
            def _():
                down_s[batch] = total(n, 0)

        else:
            partner_rows(n, slot, 0)
            my_rows(n, slot, 0)
            up_s[batch] = total(n, 0)

            @pl.when(s > 0)
            def _():
                x_copy(up_s.at[batch], n, above).start()

            out_ref[batch] = down_s[batch] + up_s[batch]

    offset = TURN + (slabs - 1 - s) * GAP
    bodies = {"inject": inject, "spread": spread, "finish": finish}
    keep = DONE - SPREAD + 1
    items = 2 * row_blocks
    each = items // DONE

    @pl.when(s > 0)
    def _():
        lax.fori_loop(0, items, prepare, 0)

    def round_body(step, carry):
        for kind, way, delay in ROUND:
            if kind == "prepare":

                @pl.when((s == 0) & (step < DONE))
                def _():
                    lax.fori_loop(step * each, step * each + each, prepare, 0)

                continue
            is_down = way == "down"
            batch = step - delay - (0 if is_down else offset)

            @pl.when((batch >= 0) & (batch < batches))
            def _():
                slot = lax.rem(batch, keep) + (0 if is_down else keep)
                bodies[kind](batch + (0 if is_down else batches), batch, slot, is_down)

        return carry

    lax.fori_loop(0, batches + offset + DONE, round_body, 0)

    def drain(n, carry):
        sent = gat.at[n, pl.ds(0, PIECES - 1)]
        pltpu.make_async_copy(sent, sent, tree_send.at[n]).wait()
        ex_copy(n, 0).wait_send()

        @pl.when(n < batches)
        def _():
            ex_copy(n, 1).wait_send()

        @pl.when(((n < batches) & (s < slabs - 1)) | ((n >= batches) & (s > 0)))
        def _():
            x_copy(up_s.at[0], n, above).wait_send()

        return carry

    lax.fori_loop(0, 2 * batches, drain, 0)


def shards(slabs, sources, tr_vals, tr_cols, rf_vals, rf_cols):
    source = sources[0, 0, 0]
    rows_in, span = source.shape
    row_blocks, picks = tr_cols.shape[-2:]
    blocks = rows_in // BLOCK
    batches = BATCHES
    width = span // batches
    rows = blocks * width
    tasks = 2 * batches
    f32, bf16 = jnp.float32, jnp.bfloat16
    vmem = pl.BlockSpec(memory_space=pltpu.VMEM)
    smem = pl.BlockSpec(memory_space=pltpu.SMEM)
    hbm = pl.BlockSpec(memory_space=pl.ANY)
    dma = pltpu.SemaphoreType.DMA
    out = pl.pallas_call(
        functools.partial(kernel, (batches, width, blocks, row_blocks, picks, slabs)),
        out_shape=jax.ShapeDtypeStruct((batches, rows, BLOCK), f32),
        in_specs=[vmem, hbm, hbm, smem, smem],
        out_specs=vmem,
        scratch_shapes=[
            pltpu.VMEM((tasks, PIECES, rows, BLOCK), f32),
            pltpu.VMEM((2 * (DONE - SPREAD + 1), PIECES * blocks, 2 * width, BLOCK), bf16),
            pltpu.VMEM((2 * row_blocks, 2 * BLOCK, picks * BLOCK), bf16),
            pltpu.VMEM((2 * row_blocks, picks, BLOCK, BLOCK), f32),
            pltpu.VMEM((batches, rows, BLOCK), f32),
            pltpu.VMEM((tasks, rows, BLOCK), f32),
            pltpu.VMEM((batches, rows, BLOCK), f32),
            pltpu.VMEM((batches, rows, BLOCK), f32),
            pltpu.VMEM((batches, rows, BLOCK), f32),
            pltpu.VMEM((2, rows, BLOCK), f32),
            pltpu.VMEM((tasks, 2, rows, BLOCK), f32),
            pltpu.VMEM((tasks, 2, rows, BLOCK), f32),
            pltpu.SMEM((2, row_blocks, picks), jnp.int32),
            dma((2 * row_blocks,)),
            dma((tasks,)),
            dma((tasks, RING - 1)),
            dma((tasks,)),
            dma((tasks, 2)),
            dma((tasks, 2)),
            dma((tasks,)),
            dma((tasks,)),
        ],
        compiler_params=pltpu.CompilerParams(
            collective_id=0,
            has_side_effects=True,
            vmem_limit_bytes=60 * 1024 * 1024,
        ),
    )(source, tr_vals[0, 0, 0], rf_vals[0, 0, 0], tr_cols[0, 0, 0], rf_cols[0, 0, 0])
    out = out.reshape(batches, blocks, width, BLOCK).transpose(1, 3, 0, 2)
    return out.reshape(rows_in, span)[None, None, None]


def solution(mesh):
    placed = (
        P("slab", "col", "row", None, None),
        P("slab", "col", "row", None, None, None, None),
        P("slab", "col", "row", None, None),
        P("slab", "col", "row", None, None, None, None),
        P("slab", "col", "row", None, None),
    )
    return jax.shard_map(
        functools.partial(shards, mesh.shape["slab"]),
        mesh=mesh,
        in_specs=placed,
        out_specs=P("slab", "col", "row", None, None),
        check_vma=False,
    )
```

```python
import functools

import jax
import jax.numpy as jnp
from jax import lax
from jax.experimental import pallas as pl
from jax.experimental.pallas import tpu as pltpu
from jax.sharding import PartitionSpec as P

MESH = pl.DeviceIdType.MESH
BATCHES = 8
RING = 4
PIECES = RING * RING
BLOCK = 128
SPREAD = 1
DONE = 2
TURN = 2
GAP = 5
ROUND = (
    ("spread", "down", SPREAD),
    ("spread", "up", SPREAD),
    ("inject", "down", 0),
    ("prepare", "", 0),
    ("finish", "down", DONE),
    ("inject", "up", 0),
    ("finish", "up", DONE),
)


def kernel(
    dims,
    src_ref,
    trv_ref,
    rfv_ref,
    trc_ref,
    rfc_ref,
    out_ref,
    gat,
    xs,
    wts,
    stage,
    src_t,
    out_t,
    xrecv,
    down_s,
    refl_s,
    up_s,
    own,
    ex_src,
    ex_dst,
    cols,
    load_sem,
    first_recv,
    second_recv,
    tree_send,
    ex_recv,
    ex_send,
    x_recv,
    x_send,
):
    batches, width, blocks, row_blocks, picks, slabs = dims
    own_rows = row_blocks // 2
    s = lax.axis_index("slab")
    r = lax.axis_index("row")
    c = lax.axis_index("col")
    y = lax.rem(c, RING)
    z = lax.div(c, RING)
    a = y * (1 - r) + z * r
    b = z * (1 - r) + y * r
    step_a = 1 + (RING - 1) * r
    step_b = RING - (RING - 1) * r

    def col(da, db):
        return lax.rem(a + da + RING, RING) * step_a + lax.rem(b + db + RING, RING) * step_b

    def plane(da, db):
        return (s, r, col(da, db))

    partner = (s, 1 - r, c)
    below = (lax.rem(s + 1, slabs), r, c)
    above = (lax.rem(s + slabs - 1, slabs), r, c)

    def load(op, i):
        ref = trv_ref if op == 0 else rfv_ref
        return pltpu.make_async_copy(ref.at[i], stage.at[op * row_blocks + i], load_sem.at[op * row_blocks + i])

    for op in range(2):
        for i in range(row_blocks):
            load(op, i).start()

    barrier = pltpu.get_barrier_semaphore()
    near = [plane(d, 0) for d in (1, 2, -1)] + [plane(0, d) for d in (1, 2, -1)]
    greeted = (*near, partner, below, above)
    for device in greeted:
        pl.semaphore_signal(barrier, inc=1, device_id=device, device_id_type=MESH)

    for j in range(blocks):
        turned = jnp.transpose(src_ref[j * BLOCK : (j + 1) * BLOCK, :])
        for n in range(batches):
            src_t[n, j * width : (j + 1) * width, :] = turned[n * width : (n + 1) * width, :]

    pl.semaphore_wait(barrier, len(greeted))

    mine = b * RING

    def tree(source, target, n, device, arrival):
        pltpu.make_async_remote_copy(
            src_ref=source,
            dst_ref=target,
            send_sem=tree_send.at[n],
            recv_sem=arrival,
            device_id=device,
            device_id_type=MESH,
        ).start()

    def arrived(n, count, semaphore):
        some = gat.at[n, pl.ds(0, count)]
        pltpu.make_async_copy(some, some, semaphore).wait()

    def split(n, slot, group):
        for p in range(RING):
            at = group * RING + p
            to = (lax.rem(a + p, RING) * step_a + group * step_b) * blocks
            for j in range(blocks):
                value = gat[n, at, j * width : (j + 1) * width, :]
                high = value.astype(jnp.bfloat16)
                xs[slot, to + j, 0:width, :] = high
                xs[slot, to + j, width : 2 * width, :] = (value - high.astype(jnp.float32)).astype(jnp.bfloat16)

    def x_copy(source, n, device):
        return pltpu.make_async_remote_copy(
            src_ref=source,
            dst_ref=xrecv.at[n],
            send_sem=x_send.at[n],
            recv_sem=x_recv.at[n],
            device_id=device,
            device_id_type=MESH,
        )

    def inject(n, batch, slot, is_down):
        held = src_t if is_down else refl_s
        end = 0 if is_down else slabs - 1

        @pl.when(s == end)
        def _():
            gat[n, mine] = held[batch]

        @pl.when(s != end)
        def _():
            x_copy(xrecv.at[n], n, above).wait_recv()
            gat[n, mine] = held[batch] + xrecv[n]

        own_piece = gat.at[n, mine]
        for da in (2, 1, -1):
            tree(own_piece, gat.at[n, mine + (RING - da) % RING], n, plane(da, 0), first_recv.at[n])
        for order, db in enumerate((2, 1, -1)):
            tree(own_piece, own_piece, n, plane(0, db), second_recv.at[n, order])

    def spread(n, batch, slot, is_down):
        arrived(n, RING - 1, first_recv.at[n])
        others = gat.at[n, pl.ds(mine + 1, RING - 1)]
        for order, db in enumerate((2, 1, -1)):
            tree(others, others, n, plane(0, db), second_recv.at[n, order])
        split(n, slot, b)

    def prepare(item, carry):
        pltpu.make_async_copy(trv_ref.at[0], stage.at[item], load_sem.at[item]).wait()
        for k in range(picks):
            value = jnp.transpose(stage[item, k])
            high = value.astype(jnp.bfloat16)
            low = (value - high.astype(jnp.float32)).astype(jnp.bfloat16)
            wts[item, k * BLOCK : (k + 1) * BLOCK, 0:BLOCK] = high
            wts[item, k * BLOCK : (k + 1) * BLOCK, BLOCK : 2 * BLOCK] = low
        return carry

    def ex_copy(n, op):
        return pltpu.make_async_remote_copy(
            src_ref=ex_src.at[n, op],
            dst_ref=ex_dst.at[n, op],
            send_sem=ex_send.at[n],
            recv_sem=ex_recv.at[n, op],
            device_id=partner,
            device_id_type=MESH,
        )

    def product(slot, op, i):
        picked = jnp.concatenate([xs[slot, cols[op, i, k]] for k in range(picks)], axis=1)
        full = lax.dot_general(
            picked,
            wts[op * row_blocks + i],
            (((1,), (0,)), ((), ())),
            preferred_element_type=jnp.float32,
        )
        high, low = full[:width], full[width:]
        return high[:, :BLOCK] + ((high[:, BLOCK:] + low[:, :BLOCK]) + low[:, BLOCK:])

    def partner_rows(n, slot, op):
        for j in range(own_rows):
            ex_src[n, op, j * width : (j + 1) * width, :] = product(slot, op, (1 - r) * own_rows + j)
        ex_copy(n, op).start()

    def my_rows(slot, op):
        for j in range(own_rows):
            own[op, j * width : (j + 1) * width, :] = product(slot, op, r * own_rows + j)

    def total(n, op):
        ex_copy(n, op).wait_recv()
        return own[op] + ex_dst[n, op]

    def finish(n, batch, slot, is_down):
        for order, db in ((1, 1), (2, -1), (0, 2)):
            arrived(n, RING, second_recv.at[n, order])
            split(n, slot, lax.rem(b - db + RING, RING))
        if is_down:
            first = lax.div(s, slabs - 1)
            second = 1 - first
            partner_rows(n, slot, first)
            my_rows(slot, first)
            partner_rows(n, slot, second)

            @pl.when(s < slabs - 1)
            def _():
                down_s[batch] = total(n, 0)
                x_copy(down_s.at[batch], n, below).start()

            @pl.when(s == slabs - 1)
            def _():
                refl_s[batch] = total(n, 1)

            my_rows(slot, second)

            @pl.when(s < slabs - 1)
            def _():
                refl_s[batch] = total(n, 1)

            @pl.when(s == slabs - 1)
            def _():
                down_s[batch] = total(n, 0)

        else:
            partner_rows(n, slot, 0)
            my_rows(slot, 0)
            up_s[batch] = total(n, 0)

            @pl.when(s > 0)
            def _():
                x_copy(up_s.at[batch], n, above).start()

            start = pl.ds(pl.multiple_of(batch * width, width), width)
            for j in range(blocks):
                at = pl.ds(j * width, width)
                out_t[j, start, :] = down_s[batch, at, :] + up_s[batch, at, :]

    offset = TURN + (slabs - 1 - s) * GAP
    bodies = {"inject": inject, "spread": spread, "finish": finish}
    keep = DONE - SPREAD + 1
    items = 2 * row_blocks
    each = items // DONE

    def tables():
        for i in range(row_blocks):
            for k in range(picks):
                cols[0, i, k] = trc_ref[i, 0, k]
                cols[1, i, k] = rfc_ref[i, 0, k]

    @pl.when(s > 0)
    def _():
        lax.fori_loop(0, items, prepare, 0)

    def round_body(step, carry):
        for kind, way, delay in ROUND:
            if kind == "prepare":

                pl.when(step == 0)(tables)

                @pl.when((s == 0) & (step < DONE))
                def _():
                    lax.fori_loop(step * each, step * each + each, prepare, 0)

                continue
            is_down = way == "down"
            batch = step - delay - (0 if is_down else offset)

            @pl.when((batch >= 0) & (batch < batches))
            def _():
                slot = lax.rem(batch, keep) + (0 if is_down else keep)
                bodies[kind](batch + (0 if is_down else batches), batch, slot, is_down)

        return carry

    lax.fori_loop(0, batches + offset + DONE, round_body, 0)

    for j in range(blocks):
        out_ref[j * BLOCK : (j + 1) * BLOCK, :] = jnp.transpose(out_t[j])

    def drain(n, carry):
        is_down = n < batches
        sent = gat.at[n, pl.ds(0, PIECES - 1)]
        pltpu.make_async_copy(sent, sent, tree_send.at[n]).wait()

        @pl.when(is_down)
        def _():
            pltpu.make_async_copy(ex_src.at[n], ex_src.at[n], ex_send.at[n]).wait()

        @pl.when(jnp.logical_not(is_down))
        def _():
            ex_copy(n, 0).wait_send()

        @pl.when((is_down & (s < slabs - 1)) | (jnp.logical_not(is_down) & (s > 0)))
        def _():
            x_copy(up_s.at[0], n, above).wait_send()

        return carry

    lax.fori_loop(0, 2 * batches, drain, 0)


def shards(slabs, sources, tr_vals, tr_cols, rf_vals, rf_cols):
    source = sources[0, 0, 0]
    rows_in, span = source.shape
    row_blocks, picks = tr_cols.shape[-2:]
    blocks = rows_in // BLOCK
    batches = BATCHES
    width = span // batches
    rows = blocks * width
    tasks = 2 * batches
    f32, bf16 = jnp.float32, jnp.bfloat16
    vmem = pl.BlockSpec(memory_space=pltpu.VMEM)
    smem = pl.BlockSpec(memory_space=pltpu.SMEM)
    hbm = pl.BlockSpec(memory_space=pl.ANY)
    dma = pltpu.SemaphoreType.DMA
    out = pl.pallas_call(
        functools.partial(kernel, (batches, width, blocks, row_blocks, picks, slabs)),
        out_shape=jax.ShapeDtypeStruct((rows_in, span), f32),
        in_specs=[vmem, hbm, hbm, smem, smem],
        out_specs=vmem,
        scratch_shapes=[
            pltpu.VMEM((tasks, PIECES, rows, BLOCK), f32),
            pltpu.VMEM((2 * (DONE - SPREAD + 1), PIECES * blocks, 2 * width, BLOCK), bf16),
            pltpu.VMEM((2 * row_blocks, picks * BLOCK, 2 * BLOCK), bf16),
            pltpu.VMEM((2 * row_blocks, picks, BLOCK, BLOCK), f32),
            pltpu.VMEM((batches, rows, BLOCK), f32),
            pltpu.VMEM((blocks, span, BLOCK), f32),
            pltpu.VMEM((tasks, rows, BLOCK), f32),
            pltpu.VMEM((batches, rows, BLOCK), f32),
            pltpu.VMEM((batches, rows, BLOCK), f32),
            pltpu.VMEM((batches, rows, BLOCK), f32),
            pltpu.VMEM((2, rows, BLOCK), f32),
            pltpu.VMEM((tasks, 2, rows, BLOCK), f32),
            pltpu.VMEM((tasks, 2, rows, BLOCK), f32),
            pltpu.SMEM((2, row_blocks, picks), jnp.int32),
            dma((2 * row_blocks,)),
            dma((tasks,)),
            dma((tasks, RING - 1)),
            dma((tasks,)),
            dma((tasks, 2)),
            dma((tasks,)),
            dma((tasks,)),
            dma((tasks,)),
        ],
        compiler_params=pltpu.CompilerParams(
            collective_id=0,
            has_side_effects=True,
            vmem_limit_bytes=60 * 1024 * 1024,
        ),
    )(source, tr_vals[0, 0, 0], rf_vals[0, 0, 0], tr_cols[0, 0, 0][:, None], rf_cols[0, 0, 0][:, None])
    return out[None, None, None]


def solution(mesh):
    placed = (
        P("slab", "col", "row", None, None),
        P("slab", "col", "row", None, None, None, None),
        P("slab", "col", "row", None, None),
        P("slab", "col", "row", None, None, None, None),
        P("slab", "col", "row", None, None),
    )
    return jax.shard_map(
        functools.partial(shards, mesh.shape["slab"]),
        mesh=mesh,
        in_specs=placed,
        out_specs=P("slab", "col", "row", None, None),
        check_vma=False,
    )
```

```python
import functools

import jax
import jax.numpy as jnp
from jax import lax
from jax.experimental import pallas as pl
from jax.experimental.pallas import tpu as pltpu
from jax.sharding import PartitionSpec as P

MESH = pl.DeviceIdType.MESH
BATCHES = 16
RING = 4
PIECES = RING * RING
BLOCK = 128
RELAYED = False
TURN = 4
GAP = 8
KEEP = 3
OTHERS = (
    ("inject", "down", 0),
    ("spread", "down", 1),
    ("inject", "up", 0),
    ("spread", "up", 1),
    ("finish", "up", 3),
    ("finish", "down", 2),
)
LAST = (
    ("inject", "up", 0),
    ("finish", "down", 3),
    ("inject", "down", 0),
    ("spread", "down", 1),
    ("spread", "up", 1),
    ("finish", "up", 3),
)


def kernel(
    dims,
    src_ref,
    trv_ref,
    rfv_ref,
    trc_ref,
    rfc_ref,
    out_ref,
    gat,
    xs,
    wts,
    stage,
    src_t,
    out_t,
    xrecv,
    down_s,
    refl_s,
    up_s,
    own,
    ex_src,
    ex_dst,
    cols,
    load_sem,
    first_recv,
    second_recv,
    tree_send,
    ex_recv,
    ex_send,
    x_recv,
    x_send,
):
    batches, width, blocks, row_blocks, picks, slabs = dims
    own_rows = row_blocks // 2
    s = lax.axis_index("slab")
    r = lax.axis_index("row")
    c = lax.axis_index("col")
    y = lax.rem(c, RING)
    z = lax.div(c, RING)
    a = y * (1 - r) + z * r
    b = z * (1 - r) + y * r
    step_a = 1 + (RING - 1) * r
    step_b = RING - (RING - 1) * r

    def col(da, db):
        return lax.rem(a + da + RING, RING) * step_a + lax.rem(b + db + RING, RING) * step_b

    def plane(da, db):
        return (s, r, col(da, db))

    partner = (s, 1 - r, c)
    below = (lax.rem(s + 1, slabs), r, c)
    above = (lax.rem(s + slabs - 1, slabs), r, c)

    def load(op, i):
        ref = trv_ref if op == 0 else rfv_ref
        return pltpu.make_async_copy(ref.at[i], stage.at[op * row_blocks + i], load_sem.at[op * row_blocks + i])

    for op in range(2):
        for i in range(row_blocks):
            load(op, i).start()

    barrier = pltpu.get_barrier_semaphore()
    near = [plane(d, 0) for d in (1, 2, -1)] + [plane(0, d) for d in (1, 2, -1)]
    greeted = (*near, partner, below, above)
    for device in greeted:
        pl.semaphore_signal(barrier, inc=1, device_id=device, device_id_type=MESH)

    for j in range(blocks):
        turned = jnp.transpose(src_ref[j * BLOCK : (j + 1) * BLOCK, :])
        for n in range(batches):
            src_t[n, j * width : (j + 1) * width, :] = turned[n * width : (n + 1) * width, :]

    pl.semaphore_wait(barrier, len(greeted))

    mine = b * RING

    def tree(source, target, n, device, arrival):
        pltpu.make_async_remote_copy(
            src_ref=source,
            dst_ref=target,
            send_sem=tree_send.at[n],
            recv_sem=arrival,
            device_id=device,
            device_id_type=MESH,
        ).start()

    def arrived(n, count, semaphore):
        some = gat.at[n, pl.ds(0, count)]
        pltpu.make_async_copy(some, some, semaphore).wait()

    def split(n, slot, group):
        for p in range(RING):
            at = group * RING + p
            to = (lax.rem(a + p, RING) * step_a + group * step_b) * blocks
            for j in range(blocks):
                value = gat[n, at, j * width : (j + 1) * width, :]
                high = value.astype(jnp.bfloat16)
                xs[slot, to + j, 0:width, :] = high
                xs[slot, to + j, width : 2 * width, :] = (value - high.astype(jnp.float32)).astype(jnp.bfloat16)

    def to_second(pieces, n):
        @pl.when((s < slabs - 1) | (not RELAYED))
        def _():
            tree(pieces, pieces, n, plane(0, 2), second_recv.at[n, 0])

        for order, db in ((1, 1), (2, -1)):
            tree(pieces, pieces, n, plane(0, db), second_recv.at[n, order])

    def x_copy(source, n, device):
        return pltpu.make_async_remote_copy(
            src_ref=source,
            dst_ref=xrecv.at[n],
            send_sem=x_send.at[n],
            recv_sem=x_recv.at[n],
            device_id=device,
            device_id_type=MESH,
        )

    def inject(n, batch, slot, is_down):
        held = src_t if is_down else refl_s
        end = 0 if is_down else slabs - 1

        @pl.when(s == end)
        def _():
            gat[n, mine] = held[batch]

        @pl.when(s != end)
        def _():
            x_copy(xrecv.at[n], n, above).wait_recv()
            gat[n, mine] = held[batch] + xrecv[n]

        own_piece = gat.at[n, mine]
        for da in (2, 1, -1):
            tree(own_piece, gat.at[n, mine + (RING - da) % RING], n, plane(da, 0), first_recv.at[n])
        to_second(own_piece, n)

    def spread(n, batch, slot, is_down):
        arrived(n, RING - 1, first_recv.at[n])
        others = gat.at[n, pl.ds(mine + 1, RING - 1)]
        to_second(others, n)
        split(n, slot, b)

    def relay(n, batch, slot, is_down):
        @pl.when(s == slabs - 1)
        def _():
            for order, db in ((1, 1), (2, -1)):
                arrived(n, RING, second_recv.at[n, order])
                group = lax.rem(b - db + RING, RING)
                passed = gat.at[n, pl.ds(group * RING + (order - 1) * RING // 2, RING // 2)]
                tree(passed, passed, n, plane(0, db), second_recv.at[n, 0])
            for db in (1, -1):
                split(n, slot, lax.rem(b - db + RING, RING))

    def prepare(item, carry):
        pltpu.make_async_copy(trv_ref.at[0], stage.at[item], load_sem.at[item]).wait()
        for k in range(picks):
            value = jnp.transpose(stage[item, k])
            high = value.astype(jnp.bfloat16)
            low = (value - high.astype(jnp.float32)).astype(jnp.bfloat16)
            wts[item, k * BLOCK : (k + 1) * BLOCK, 0:BLOCK] = high
            wts[item, k * BLOCK : (k + 1) * BLOCK, BLOCK : 2 * BLOCK] = low
        return carry

    def ex_copy(n, op):
        return pltpu.make_async_remote_copy(
            src_ref=ex_src.at[n, op],
            dst_ref=ex_dst.at[n, op],
            send_sem=ex_send.at[n],
            recv_sem=ex_recv.at[n, op],
            device_id=partner,
            device_id_type=MESH,
        )

    def product(slot, op, i):
        picked = jnp.concatenate([xs[slot, cols[op, i, k]] for k in range(picks)], axis=1)
        full = lax.dot_general(
            picked,
            wts[op * row_blocks + i],
            (((1,), (0,)), ((), ())),
            preferred_element_type=jnp.float32,
        )
        high, low = full[:width], full[width:]
        return high[:, :BLOCK] + ((high[:, BLOCK:] + low[:, :BLOCK]) + low[:, BLOCK:])

    def partner_rows(n, slot, op):
        for j in range(own_rows):
            ex_src[n, op, j * width : (j + 1) * width, :] = product(slot, op, (1 - r) * own_rows + j)
        ex_copy(n, op).start()

    def my_rows(slot, op):
        for j in range(own_rows):
            own[op, j * width : (j + 1) * width, :] = product(slot, op, r * own_rows + j)

    def total(n, op):
        ex_copy(n, op).wait_recv()
        return own[op] + ex_dst[n, op]

    def finish(n, batch, slot, is_down):
        @pl.when((s < slabs - 1) | (not RELAYED))
        def _():
            for order, db in ((1, 1), (2, -1)):
                arrived(n, RING, second_recv.at[n, order])
                split(n, slot, lax.rem(b - db + RING, RING))

        arrived(n, RING, second_recv.at[n, 0])
        split(n, slot, lax.rem(b + 2, RING))
        if is_down:
            first = lax.div(s, slabs - 1)
            second = 1 - first
            partner_rows(n, slot, first)
            my_rows(slot, first)
            partner_rows(n, slot, second)

            @pl.when(s < slabs - 1)
            def _():
                down_s[batch] = total(n, 0)
                x_copy(down_s.at[batch], n, below).start()

            @pl.when(s == slabs - 1)
            def _():
                refl_s[batch] = total(n, 1)

            my_rows(slot, second)

            @pl.when(s < slabs - 1)
            def _():
                refl_s[batch] = total(n, 1)

            @pl.when(s == slabs - 1)
            def _():
                down_s[batch] = total(n, 0)

        else:
            partner_rows(n, slot, 0)
            my_rows(slot, 0)
            up_s[batch] = total(n, 0)

            @pl.when(s > 0)
            def _():
                x_copy(up_s.at[batch], n, above).start()

            start = pl.ds(pl.multiple_of(batch * width, width), width)
            for j in range(blocks):
                at = pl.ds(j * width, width)
                out_t[j, start, :] = down_s[batch, at, :] + up_s[batch, at, :]

    offset = TURN + (slabs - 1 - s) * GAP
    bodies = {"inject": inject, "spread": spread, "relay": relay, "finish": finish}
    items = 2 * row_blocks
    each = items // 2
    longest = max(delay for _, _, delay in OTHERS + LAST)

    def tables():
        for i in range(row_blocks):
            for k in range(picks):
                cols[0, i, k] = trc_ref[i, 0, k]
                cols[1, i, k] = rfc_ref[i, 0, k]

    @pl.when(s > 0)
    def _():
        tables()
        lax.fori_loop(0, items, prepare, 0)

    def round_body(order, step, carry):
        for kind, way, delay in order:
            is_down = way == "down"
            batch = step - delay - (0 if is_down else offset)

            @pl.when((batch >= 0) & (batch < batches))
            def _():
                slot = lax.rem(batch, KEEP) + (0 if is_down else KEEP)
                bodies[kind](batch + (0 if is_down else batches), batch, slot, is_down)

        @pl.when((s == 0) & (step < 2))
        def _():
            pl.when(step == 0)(tables)
            lax.fori_loop(step * each, step * each + each, prepare, 0)

        return carry

    for order, here in ((OTHERS, s < slabs - 1), (LAST, s == slabs - 1)):

        @pl.when(here)
        def _():
            lax.fori_loop(0, batches + offset + longest, functools.partial(round_body, order), 0)

    for j in range(blocks):
        out_ref[j * BLOCK : (j + 1) * BLOCK, :] = jnp.transpose(out_t[j])

    def drain(n, carry):
        is_down = n < batches
        sent = gat.at[n, pl.ds(0, PIECES - 1)]
        pltpu.make_async_copy(sent, sent, tree_send.at[n]).wait()

        @pl.when(is_down)
        def _():
            pltpu.make_async_copy(ex_src.at[n], ex_src.at[n], ex_send.at[n]).wait()

        @pl.when(jnp.logical_not(is_down))
        def _():
            ex_copy(n, 0).wait_send()

        @pl.when((is_down & (s < slabs - 1)) | (jnp.logical_not(is_down) & (s > 0)))
        def _():
            x_copy(up_s.at[0], n, above).wait_send()

        return carry

    lax.fori_loop(0, 2 * batches, drain, 0)


def shards(slabs, sources, tr_vals, tr_cols, rf_vals, rf_cols):
    source = sources[0, 0, 0]
    rows_in, span = source.shape
    row_blocks, picks = tr_cols.shape[-2:]
    blocks = rows_in // BLOCK
    batches = BATCHES
    width = span // batches
    rows = blocks * width
    tasks = 2 * batches
    f32, bf16 = jnp.float32, jnp.bfloat16
    vmem = pl.BlockSpec(memory_space=pltpu.VMEM)
    smem = pl.BlockSpec(memory_space=pltpu.SMEM)
    hbm = pl.BlockSpec(memory_space=pl.ANY)
    dma = pltpu.SemaphoreType.DMA
    out = pl.pallas_call(
        functools.partial(kernel, (batches, width, blocks, row_blocks, picks, slabs)),
        out_shape=jax.ShapeDtypeStruct((rows_in, span), f32),
        in_specs=[vmem, hbm, hbm, smem, smem],
        out_specs=vmem,
        scratch_shapes=[
            pltpu.VMEM((tasks, PIECES, rows, BLOCK), f32),
            pltpu.VMEM((2 * KEEP, PIECES * blocks, 2 * width, BLOCK), bf16),
            pltpu.VMEM((2 * row_blocks, picks * BLOCK, 2 * BLOCK), bf16),
            pltpu.VMEM((2 * row_blocks, picks, BLOCK, BLOCK), f32),
            pltpu.VMEM((batches, rows, BLOCK), f32),
            pltpu.VMEM((blocks, span, BLOCK), f32),
            pltpu.VMEM((tasks, rows, BLOCK), f32),
            pltpu.VMEM((batches, rows, BLOCK), f32),
            pltpu.VMEM((batches, rows, BLOCK), f32),
            pltpu.VMEM((batches, rows, BLOCK), f32),
            pltpu.VMEM((2, rows, BLOCK), f32),
            pltpu.VMEM((tasks, 2, rows, BLOCK), f32),
            pltpu.VMEM((tasks, 2, rows, BLOCK), f32),
            pltpu.SMEM((2, row_blocks, picks), jnp.int32),
            dma((2 * row_blocks,)),
            dma((tasks,)),
            dma((tasks, RING - 1)),
            dma((tasks,)),
            dma((tasks, 2)),
            dma((tasks,)),
            dma((tasks,)),
            dma((tasks,)),
        ],
        compiler_params=pltpu.CompilerParams(
            collective_id=0,
            has_side_effects=True,
            vmem_limit_bytes=60 * 1024 * 1024,
        ),
    )(source, tr_vals[0, 0, 0], rf_vals[0, 0, 0], tr_cols[0, 0, 0][:, None], rf_cols[0, 0, 0][:, None])
    return out[None, None, None]


def solution(mesh):
    placed = (
        P("slab", "col", "row", None, None),
        P("slab", "col", "row", None, None, None, None),
        P("slab", "col", "row", None, None),
        P("slab", "col", "row", None, None, None, None),
        P("slab", "col", "row", None, None),
    )
    return jax.shard_map(
        functools.partial(shards, mesh.shape["slab"]),
        mesh=mesh,
        in_specs=placed,
        out_specs=P("slab", "col", "row", None, None),
        check_vma=False,
    )
```

```python
import functools

import jax
import jax.numpy as jnp
from jax import lax
from jax.experimental import pallas as pl
from jax.experimental.pallas import tpu as pltpu
from jax.sharding import PartitionSpec as P

MESH = pl.DeviceIdType.MESH
BATCHES = 16
RING = 4
PIECES = RING * RING
BLOCK = 128
TURN = 4
GAP = 8
KEEP = 3
OTHERS = (
    ("inject", "down", 0),
    ("spread", "down", 1),
    ("settle", "down", 3),
    ("inject", "up", 0),
    ("spread", "up", 1),
    ("finish", "up", 3),
    ("settle", "up", 3),
    ("finish", "down", 2),
)
LAST = (
    ("inject", "up", 0),
    ("finish", "down", 3),
    ("inject", "down", 0),
    ("spread", "down", 1),
    ("settle", "down", 3),
    ("spread", "up", 1),
    ("finish", "up", 3),
    ("settle", "up", 3),
)


def kernel(
    dims,
    src_ref,
    trv_ref,
    rfv_ref,
    trc_ref,
    rfc_ref,
    out_ref,
    gat,
    xs,
    wts,
    stage,
    src_t,
    out_t,
    xrecv,
    down_s,
    refl_s,
    up_s,
    own,
    ex_src,
    ex_dst,
    cols,
    load_sem,
    first_recv,
    second_recv,
    tree_send,
    ex_recv,
    ex_send,
    x_recv,
    x_send,
):
    batches, width, blocks, row_blocks, picks, slabs = dims
    own_rows = row_blocks // 2
    s = lax.axis_index("slab")
    r = lax.axis_index("row")
    c = lax.axis_index("col")
    y = lax.rem(c, RING)
    z = lax.div(c, RING)
    a = y * (1 - r) + z * r
    b = z * (1 - r) + y * r
    step_a = 1 + (RING - 1) * r
    step_b = RING - (RING - 1) * r

    def col(da, db):
        return lax.rem(a + da + RING, RING) * step_a + lax.rem(b + db + RING, RING) * step_b

    def plane(da, db):
        return (s, r, col(da, db))

    partner = (s, 1 - r, c)
    below = (lax.rem(s + 1, slabs), r, c)
    above = (lax.rem(s + slabs - 1, slabs), r, c)

    def load(op, i):
        ref = trv_ref if op == 0 else rfv_ref
        return pltpu.make_async_copy(ref.at[i], stage.at[op * row_blocks + i], load_sem.at[op * row_blocks + i])

    for op in range(2):
        for i in range(row_blocks):
            load(op, i).start()

    barrier = pltpu.get_barrier_semaphore()
    near = [plane(d, 0) for d in (1, 2, -1)] + [plane(0, d) for d in (1, 2, -1)]
    greeted = (*near, partner, below, above)
    for device in greeted:
        pl.semaphore_signal(barrier, inc=1, device_id=device, device_id_type=MESH)

    for j in range(blocks):
        turned = jnp.transpose(src_ref[j * BLOCK : (j + 1) * BLOCK, :])
        for n in range(batches):
            src_t[n, j * width : (j + 1) * width, :] = turned[n * width : (n + 1) * width, :]

    pl.semaphore_wait(barrier, len(greeted))

    mine = b * RING

    def tree(source, target, n, device, arrival):
        pltpu.make_async_remote_copy(
            src_ref=source,
            dst_ref=target,
            send_sem=tree_send.at[n],
            recv_sem=arrival,
            device_id=device,
            device_id_type=MESH,
        ).start()

    def arrived(n, count, semaphore):
        some = gat.at[n, pl.ds(0, count)]
        pltpu.make_async_copy(some, some, semaphore).wait()

    def split(n, slot, group):
        for p in range(RING):
            at = group * RING + p
            to = (lax.rem(a + p, RING) * step_a + group * step_b) * blocks
            for j in range(blocks):
                value = gat[n, at, j * width : (j + 1) * width, :]
                high = value.astype(jnp.bfloat16)
                xs[slot, to + j, 0:width, :] = high
                xs[slot, to + j, width : 2 * width, :] = (value - high.astype(jnp.float32)).astype(jnp.bfloat16)

    def to_second(pieces, n):
        for order, db in ((1, 1), (2, -1), (0, 2)):
            tree(pieces, pieces, n, plane(0, db), second_recv.at[n, order])

    def x_copy(source, n, device):
        return pltpu.make_async_remote_copy(
            src_ref=source,
            dst_ref=xrecv.at[n],
            send_sem=x_send.at[n],
            recv_sem=x_recv.at[n],
            device_id=device,
            device_id_type=MESH,
        )

    def inject(n, batch, slot, is_down):
        held = src_t if is_down else refl_s
        end = 0 if is_down else slabs - 1

        @pl.when(s == end)
        def _():
            gat[n, mine] = held[batch]

        @pl.when(s != end)
        def _():
            x_copy(xrecv.at[n], n, above).wait_recv()
            gat[n, mine] = held[batch] + xrecv[n]

        own_piece = gat.at[n, mine]
        for da in (2, 1, -1):
            tree(own_piece, gat.at[n, mine + (RING - da) % RING], n, plane(da, 0), first_recv.at[n])
        to_second(own_piece, n)

    def spread(n, batch, slot, is_down):
        arrived(n, RING - 1, first_recv.at[n])
        others = gat.at[n, pl.ds(mine + 1, RING - 1)]
        to_second(others, n)
        split(n, slot, b)

    def to_second(pieces, n):
        for order, db in ((1, 1), (2, -1), (0, 2)):
            tree(pieces, pieces, n, plane(0, db), second_recv.at[n, order])

    def x_copy(source, n, device):
        return pltpu.make_async_remote_copy(
            src_ref=source,
            dst_ref=xrecv.at[n],
            send_sem=x_send.at[n],
            recv_sem=x_recv.at[n],
            device_id=device,
            device_id_type=MESH,
        )

    def inject(n, batch, slot, is_down):
        held = src_t if is_down else refl_s
        end = 0 if is_down else slabs - 1

        @pl.when(s == end)
        def _():
            gat[n, mine] = held[batch]

        @pl.when(s != end)
        def _():
            x_copy(xrecv.at[n], n, above).wait_recv()
            gat[n, mine] = held[batch] + xrecv[n]

        own_piece = gat.at[n, mine]
        for da in (2, 1, -1):
            tree(own_piece, gat.at[n, mine + (RING - da) % RING], n, plane(da, 0), first_recv.at[n])
        to_second(own_piece, n)

    def spread(n, batch, slot, is_down):
        arrived(n, RING - 1, first_recv.at[n])
        others = gat.at[n, pl.ds(mine + 1, RING - 1)]
        to_second(others, n)
        split(n, slot, b)

    def relay(n, batch, slot, is_down):
        @pl.when(s == slabs - 1)
        def _():
            for order, db in ((1, 1), (2, -1)):
                arrived(n, RING, second_recv.at[n, order])
                group = lax.rem(b - db + RING, RING)
                passed = gat.at[n, pl.ds(group * RING + (order - 1) * RING // 2, RING // 2)]
                tree(passed, passed, n, plane(0, db), second_recv.at[n, 0])
            for db in (1, -1):
                split(n, slot, lax.rem(b - db + RING, RING))

    def prepare(item, carry):
        pltpu.make_async_copy(trv_ref.at[0], stage.at[item], load_sem.at[item]).wait()
        for k in range(picks):
            value = jnp.transpose(stage[item, k])
            high = value.astype(jnp.bfloat16)
            low = (value - high.astype(jnp.float32)).astype(jnp.bfloat16)
            wts[item, k * BLOCK : (k + 1) * BLOCK, 0:BLOCK] = high
            wts[item, k * BLOCK : (k + 1) * BLOCK, BLOCK : 2 * BLOCK] = low
        return carry

    def ex_copy(n, op):
        return pltpu.make_async_remote_copy(
            src_ref=ex_src.at[n, op],
            dst_ref=ex_dst.at[n, op],
            send_sem=ex_send.at[n],
            recv_sem=ex_recv.at[n, op],
            device_id=partner,
            device_id_type=MESH,
        )

    def product(slot, op, i):
        picked = jnp.concatenate([xs[slot, cols[op, i, k]] for k in range(picks)], axis=1)
        full = lax.dot_general(
            picked,
            wts[op * row_blocks + i],
            (((1,), (0,)), ((), ())),
            preferred_element_type=jnp.float32,
        )
        high, low = full[:width], full[width:]
        return high[:, :BLOCK] + ((high[:, BLOCK:] + low[:, :BLOCK]) + low[:, BLOCK:])

    def partner_rows(n, slot, op):
        for j in range(own_rows):
            ex_src[n, op, j * width : (j + 1) * width, :] = product(slot, op, (1 - r) * own_rows + j)
        ex_copy(n, op).start()

    def my_rows(slot, op, keep):
        for j in range(own_rows):
            own[keep, j * width : (j + 1) * width, :] = product(slot, op, r * own_rows + j)

    def total(n, op, kept):
        ex_copy(n, op).wait_recv()
        return own[kept] + ex_dst[n, op]

    def finish(n, batch, slot, is_down):
        for order, db in ((1, 1), (2, -1), (0, 2)):
            arrived(n, RING, second_recv.at[n, order])
            split(n, slot, lax.rem(b - db + RING, RING))

        if is_down:
            first = lax.div(s, slabs - 1)
            second = 1 - first
            partner_rows(n, slot, first)
            my_rows(slot, first, 0)
            partner_rows(n, slot, second)

            @pl.when(s < slabs - 1)
            def _():
                down_s[batch] = total(n, 0, 0)
                x_copy(down_s.at[batch], n, below).start()

            @pl.when(s == slabs - 1)
            def _():
                refl_s[batch] = total(n, 1, 0)

            my_rows(slot, second, 1)
        else:
            partner_rows(n, slot, 0)
            my_rows(slot, 0, 2)

    def settle(n, batch, slot, is_down):
        if is_down:

            @pl.when(s < slabs - 1)
            def _():
                refl_s[batch] = total(n, 1, 1)

            @pl.when(s == slabs - 1)
            def _():
                down_s[batch] = total(n, 0, 1)

        else:
            up_s[batch] = total(n, 0, 2)

            @pl.when(s > 0)
            def _():
                x_copy(up_s.at[batch], n, above).start()

            start = pl.ds(pl.multiple_of(batch * width, width), width)
            for j in range(blocks):
                at = pl.ds(j * width, width)
                out_t[j, start, :] = down_s[batch, at, :] + up_s[batch, at, :]

    offset = TURN + (slabs - 1 - s) * GAP
    bodies = {"inject": inject, "spread": spread, "finish": finish, "settle": settle}
    items = 2 * row_blocks
    each = items // 2
    longest = max(delay for _, _, delay in OTHERS + LAST)

    def tables():
        for i in range(row_blocks):
            for k in range(picks):
                cols[0, i, k] = trc_ref[i, 0, k]
                cols[1, i, k] = rfc_ref[i, 0, k]

    @pl.when(s > 0)
    def _():
        tables()
        lax.fori_loop(0, items, prepare, 0)

    def round_body(order, step, carry):
        for kind, way, delay in order:
            is_down = way == "down"
            batch = step - delay - (0 if is_down else offset)

            @pl.when((batch >= 0) & (batch < batches))
            def _():
                slot = lax.rem(batch, KEEP) + (0 if is_down else KEEP)
                bodies[kind](batch + (0 if is_down else batches), batch, slot, is_down)

        @pl.when((s == 0) & (step < 2))
        def _():
            pl.when(step == 0)(tables)
            lax.fori_loop(step * each, step * each + each, prepare, 0)

        return carry

    for order, here in ((OTHERS, s < slabs - 1), (LAST, s == slabs - 1)):

        @pl.when(here)
        def _():
            lax.fori_loop(0, batches + offset + longest, functools.partial(round_body, order), 0)

    for j in range(blocks):
        out_ref[j * BLOCK : (j + 1) * BLOCK, :] = jnp.transpose(out_t[j])

    def drain(n, carry):
        is_down = n < batches
        sent = gat.at[n, pl.ds(0, PIECES - 1)]
        pltpu.make_async_copy(sent, sent, tree_send.at[n]).wait()

        @pl.when(is_down)
        def _():
            pltpu.make_async_copy(ex_src.at[n], ex_src.at[n], ex_send.at[n]).wait()

        @pl.when(jnp.logical_not(is_down))
        def _():
            ex_copy(n, 0).wait_send()

        @pl.when((is_down & (s < slabs - 1)) | (jnp.logical_not(is_down) & (s > 0)))
        def _():
            x_copy(up_s.at[0], n, above).wait_send()

        return carry

    lax.fori_loop(0, 2 * batches, drain, 0)


def shards(slabs, sources, tr_vals, tr_cols, rf_vals, rf_cols):
    source = sources[0, 0, 0]
    rows_in, span = source.shape
    row_blocks, picks = tr_cols.shape[-2:]
    blocks = rows_in // BLOCK
    batches = BATCHES
    width = span // batches
    rows = blocks * width
    tasks = 2 * batches
    f32, bf16 = jnp.float32, jnp.bfloat16
    vmem = pl.BlockSpec(memory_space=pltpu.VMEM)
    smem = pl.BlockSpec(memory_space=pltpu.SMEM)
    hbm = pl.BlockSpec(memory_space=pl.ANY)
    dma = pltpu.SemaphoreType.DMA
    out = pl.pallas_call(
        functools.partial(kernel, (batches, width, blocks, row_blocks, picks, slabs)),
        out_shape=jax.ShapeDtypeStruct((rows_in, span), f32),
        in_specs=[vmem, hbm, hbm, smem, smem],
        out_specs=vmem,
        scratch_shapes=[
            pltpu.VMEM((tasks, PIECES, rows, BLOCK), f32),
            pltpu.VMEM((2 * KEEP, PIECES * blocks, 2 * width, BLOCK), bf16),
            pltpu.VMEM((2 * row_blocks, picks * BLOCK, 2 * BLOCK), bf16),
            pltpu.VMEM((2 * row_blocks, picks, BLOCK, BLOCK), f32),
            pltpu.VMEM((batches, rows, BLOCK), f32),
            pltpu.VMEM((blocks, span, BLOCK), f32),
            pltpu.VMEM((tasks, rows, BLOCK), f32),
            pltpu.VMEM((batches, rows, BLOCK), f32),
            pltpu.VMEM((batches, rows, BLOCK), f32),
            pltpu.VMEM((batches, rows, BLOCK), f32),
            pltpu.VMEM((3, rows, BLOCK), f32),
            pltpu.VMEM((tasks, 2, rows, BLOCK), f32),
            pltpu.VMEM((tasks, 2, rows, BLOCK), f32),
            pltpu.SMEM((2, row_blocks, picks), jnp.int32),
            dma((2 * row_blocks,)),
            dma((tasks,)),
            dma((tasks, RING - 1)),
            dma((tasks,)),
            dma((tasks, 2)),
            dma((tasks,)),
            dma((tasks,)),
            dma((tasks,)),
        ],
        compiler_params=pltpu.CompilerParams(
            collective_id=0,
            has_side_effects=True,
            vmem_limit_bytes=60 * 1024 * 1024,
        ),
    )(source, tr_vals[0, 0, 0], rf_vals[0, 0, 0], tr_cols[0, 0, 0][:, None], rf_cols[0, 0, 0][:, None])
    return out[None, None, None]


def solution(mesh):
    placed = (
        P("slab", "col", "row", None, None),
        P("slab", "col", "row", None, None, None, None),
        P("slab", "col", "row", None, None),
        P("slab", "col", "row", None, None, None, None),
        P("slab", "col", "row", None, None),
    )
    return jax.shard_map(
        functools.partial(shards, mesh.shape["slab"]),
        mesh=mesh,
        in_specs=placed,
        out_specs=P("slab", "col", "row", None, None),
        check_vma=False,
    )
```

```python
import functools

import jax
import jax.numpy as jnp
from jax import lax
from jax.experimental import pallas as pl
from jax.experimental.pallas import tpu as pltpu
from jax.sharding import PartitionSpec as P

MESH = pl.DeviceIdType.MESH
BATCHES = 16
RING = 4
PIECES = RING * RING
BLOCK = 128
TURN = 4
GAP = 8
KEEP = 3
OTHERS = (
    ("inject", "down", 0),
    ("spread", "down", 1),
    ("settle", "down", 3),
    ("inject", "up", 0),
    ("spread", "up", 1),
    ("finish", "up", 3),
    ("settle", "up", 3),
    ("finish", "down", 2),
)
LAST = (
    ("inject", "up", 0),
    ("finish", "down", 3),
    ("inject", "down", 0),
    ("spread", "down", 1),
    ("settle", "down", 3),
    ("spread", "up", 1),
    ("finish", "up", 3),
    ("settle", "up", 3),
)


def kernel(
    dims,
    src_ref,
    trv_ref,
    rfv_ref,
    trc_ref,
    rfc_ref,
    out_ref,
    gat,
    xs,
    wts,
    stage,
    src_t,
    out_t,
    xrecv,
    down_s,
    refl_s,
    up_s,
    own,
    ex_src,
    ex_dst,
    cols,
    load_sem,
    first_recv,
    second_recv,
    tree_send,
    ex_recv,
    ex_send,
    x_recv,
    x_send,
):
    batches, width, blocks, row_blocks, picks, slabs = dims
    own_rows = row_blocks // 2
    s = lax.axis_index("slab")
    r = lax.axis_index("row")
    c = lax.axis_index("col")
    y = lax.rem(c, RING)
    z = lax.div(c, RING)
    a = y * (1 - r) + z * r
    b = z * (1 - r) + y * r
    step_a = 1 + (RING - 1) * r
    step_b = RING - (RING - 1) * r

    def col(da, db):
        return lax.rem(a + da + RING, RING) * step_a + lax.rem(b + db + RING, RING) * step_b

    def plane(da, db):
        return (s, r, col(da, db))

    partner = (s, 1 - r, c)
    below = (lax.rem(s + 1, slabs), r, c)
    above = (lax.rem(s + slabs - 1, slabs), r, c)

    def load(op, i):
        ref = trv_ref if op == 0 else rfv_ref
        return pltpu.make_async_copy(ref.at[i], stage.at[op * row_blocks + i], load_sem.at[op * row_blocks + i])

    for op in range(2):
        for i in range(row_blocks):
            load(op, i).start()

    barrier = pltpu.get_barrier_semaphore()
    near = [plane(d, 0) for d in (1, 2, -1)] + [plane(0, d) for d in (1, 2, -1)]
    greeted = (*near, partner, below, above)
    for device in greeted:
        pl.semaphore_signal(barrier, inc=1, device_id=device, device_id_type=MESH)

    for j in range(blocks):
        turned = jnp.transpose(src_ref[j * BLOCK : (j + 1) * BLOCK, :])
        for n in range(batches):
            src_t[n, j * width : (j + 1) * width, :] = turned[n * width : (n + 1) * width, :]

    pl.semaphore_wait(barrier, len(greeted))

    mine = b * RING

    def tree(source, target, n, device, arrival):
        pltpu.make_async_remote_copy(
            src_ref=source,
            dst_ref=target,
            send_sem=tree_send.at[lax.div(n, batches)],
            recv_sem=arrival,
            device_id=device,
            device_id_type=MESH,
        ).start()

    def arrived(n, count, semaphore):
        some = gat.at[n, pl.ds(0, count)]
        pltpu.make_async_copy(some, some, semaphore).wait()

    def split(n, slot, group):
        for p in range(RING):
            at = group * RING + p
            to = (lax.rem(a + p, RING) * step_a + group * step_b) * blocks
            for j in range(blocks):
                value = gat[n, at, j * width : (j + 1) * width, :]
                high = value.astype(jnp.bfloat16)
                xs[slot, to + j, 0:width, :] = high
                xs[slot, to + j, width : 2 * width, :] = (value - high.astype(jnp.float32)).astype(jnp.bfloat16)

    def to_second(pieces, n):
        for order, db in ((1, 1), (2, -1), (0, 2)):
            tree(pieces, pieces, n, plane(0, db), second_recv.at[n, order])

    def x_copy(source, n, device):
        return pltpu.make_async_remote_copy(
            src_ref=source,
            dst_ref=xrecv.at[n],
            send_sem=x_send,
            recv_sem=x_recv.at[n],
            device_id=device,
            device_id_type=MESH,
        )

    def inject(n, batch, slot, is_down):
        held = src_t if is_down else refl_s
        end = 0 if is_down else slabs - 1

        @pl.when(s == end)
        def _():
            gat[n, mine] = held[batch]

        @pl.when(s != end)
        def _():
            x_copy(xrecv.at[n], n, above).wait_recv()
            gat[n, mine] = held[batch] + xrecv[n]

        own_piece = gat.at[n, mine]
        for da in (2, 1, -1):
            tree(own_piece, gat.at[n, mine + (RING - da) % RING], n, plane(da, 0), first_recv.at[n])
        to_second(own_piece, n)

    def spread(n, batch, slot, is_down):
        arrived(n, RING - 1, first_recv.at[n])
        others = gat.at[n, pl.ds(mine + 1, RING - 1)]
        to_second(others, n)
        split(n, slot, b)

    def to_second(pieces, n):
        for order, db in ((1, 1), (2, -1), (0, 2)):
            tree(pieces, pieces, n, plane(0, db), second_recv.at[n, order])

    def x_copy(source, n, device):
        return pltpu.make_async_remote_copy(
            src_ref=source,
            dst_ref=xrecv.at[n],
            send_sem=x_send,
            recv_sem=x_recv.at[n],
            device_id=device,
            device_id_type=MESH,
        )

    def inject(n, batch, slot, is_down):
        held = src_t if is_down else refl_s
        end = 0 if is_down else slabs - 1

        @pl.when(s == end)
        def _():
            gat[n, mine] = held[batch]

        @pl.when(s != end)
        def _():
            x_copy(xrecv.at[n], n, above).wait_recv()
            gat[n, mine] = held[batch] + xrecv[n]

        own_piece = gat.at[n, mine]
        for da in (2, 1, -1):
            tree(own_piece, gat.at[n, mine + (RING - da) % RING], n, plane(da, 0), first_recv.at[n])
        to_second(own_piece, n)

    def spread(n, batch, slot, is_down):
        arrived(n, RING - 1, first_recv.at[n])
        others = gat.at[n, pl.ds(mine + 1, RING - 1)]
        to_second(others, n)
        split(n, slot, b)

    def relay(n, batch, slot, is_down):
        @pl.when(s == slabs - 1)
        def _():
            for order, db in ((1, 1), (2, -1)):
                arrived(n, RING, second_recv.at[n, order])
                group = lax.rem(b - db + RING, RING)
                passed = gat.at[n, pl.ds(group * RING + (order - 1) * RING // 2, RING // 2)]
                tree(passed, passed, n, plane(0, db), second_recv.at[n, 0])
            for db in (1, -1):
                split(n, slot, lax.rem(b - db + RING, RING))

    def prepare(item, carry):
        pltpu.make_async_copy(trv_ref.at[0], stage.at[item], load_sem.at[item]).wait()
        for k in range(picks):
            value = jnp.transpose(stage[item, k])
            high = value.astype(jnp.bfloat16)
            low = (value - high.astype(jnp.float32)).astype(jnp.bfloat16)
            wts[item, k * BLOCK : (k + 1) * BLOCK, 0:BLOCK] = high
            wts[item, k * BLOCK : (k + 1) * BLOCK, BLOCK : 2 * BLOCK] = low
        return carry

    def ex_copy(n, op):
        return pltpu.make_async_remote_copy(
            src_ref=ex_src.at[n, op],
            dst_ref=ex_dst.at[n, op],
            send_sem=ex_send,
            recv_sem=ex_recv.at[n, op],
            device_id=partner,
            device_id_type=MESH,
        )

    def product(slot, op, i):
        picked = jnp.concatenate([xs[slot, cols[op, i, k]] for k in range(picks)], axis=1)
        full = lax.dot_general(
            picked,
            wts[op * row_blocks + i],
            (((1,), (0,)), ((), ())),
            preferred_element_type=jnp.float32,
        )
        high, low = full[:width], full[width:]
        return high[:, :BLOCK] + ((high[:, BLOCK:] + low[:, :BLOCK]) + low[:, BLOCK:])

    def partner_rows(n, slot, op):
        for j in range(own_rows):
            ex_src[n, op, j * width : (j + 1) * width, :] = product(slot, op, (1 - r) * own_rows + j)
        ex_copy(n, op).start()

    def my_rows(slot, op, keep):
        for j in range(own_rows):
            own[keep, j * width : (j + 1) * width, :] = product(slot, op, r * own_rows + j)

    def total(n, op, kept):
        ex_copy(n, op).wait_recv()
        return own[kept] + ex_dst[n, op]

    def finish(n, batch, slot, is_down):
        for order, db in ((1, 1), (2, -1), (0, 2)):
            arrived(n, RING, second_recv.at[n, order])
            split(n, slot, lax.rem(b - db + RING, RING))

        if is_down:
            first = lax.div(s, slabs - 1)
            second = 1 - first
            partner_rows(n, slot, first)
            my_rows(slot, first, 0)
            partner_rows(n, slot, second)

            @pl.when(s < slabs - 1)
            def _():
                down_s[batch] = total(n, 0, 0)
                x_copy(down_s.at[batch], n, below).start()

            @pl.when(s == slabs - 1)
            def _():
                refl_s[batch] = total(n, 1, 0)

            my_rows(slot, second, 1)
        else:
            partner_rows(n, slot, 0)
            my_rows(slot, 0, 2)

    def settle(n, batch, slot, is_down):
        if is_down:

            @pl.when(s < slabs - 1)
            def _():
                refl_s[batch] = total(n, 1, 1)

            @pl.when(s == slabs - 1)
            def _():
                down_s[batch] = total(n, 0, 1)

        else:
            up_s[batch] = total(n, 0, 2)

            @pl.when(s > 0)
            def _():
                x_copy(up_s.at[batch], n, above).start()

            start = pl.ds(pl.multiple_of(batch * width, width), width)
            for j in range(blocks):
                at = pl.ds(j * width, width)
                out_t[j, start, :] = down_s[batch, at, :] + up_s[batch, at, :]

    offset = TURN + (slabs - 1 - s) * GAP
    bodies = {"inject": inject, "spread": spread, "finish": finish, "settle": settle}
    items = 2 * row_blocks
    each = items // 2
    longest = max(delay for _, _, delay in OTHERS + LAST)

    def tables():
        for i in range(row_blocks):
            for k in range(picks):
                cols[0, i, k] = trc_ref[i, 0, k]
                cols[1, i, k] = rfc_ref[i, 0, k]

    @pl.when(s > 0)
    def _():
        tables()
        lax.fori_loop(0, items, prepare, 0)

    def round_body(order, step, carry):
        for kind, way, delay in order:
            is_down = way == "down"
            batch = step - delay - (0 if is_down else offset)

            @pl.when((batch >= 0) & (batch < batches))
            def _():
                slot = lax.rem(batch, KEEP) + (0 if is_down else KEEP)
                bodies[kind](batch + (0 if is_down else batches), batch, slot, is_down)

        @pl.when((s == 0) & (step < 2))
        def _():
            pl.when(step == 0)(tables)
            lax.fori_loop(step * each, step * each + each, prepare, 0)

        return carry

    for order, here in ((OTHERS, s < slabs - 1), (LAST, s == slabs - 1)):

        @pl.when(here)
        def _():
            lax.fori_loop(0, batches + offset + longest, functools.partial(round_body, order), 0)

    for j in range(blocks):
        out_ref[j * BLOCK : (j + 1) * BLOCK, :] = jnp.transpose(out_t[j])

    def drained(sent, semaphore):
        pltpu.make_async_copy(sent, sent, semaphore).wait()

    for way in range(2):
        drained(gat.at[pl.ds(0, batches), pl.ds(0, PIECES - 1)], tree_send.at[way])
    drained(ex_src.at[pl.ds(0, 3 * batches // 2)], ex_send)

    @pl.when((s > 0) & (s < slabs - 1))
    def _():
        drained(xrecv, x_send)

    @pl.when((s == 0) | (s == slabs - 1))
    def _():
        drained(xrecv.at[pl.ds(0, batches)], x_send)


def shards(slabs, sources, tr_vals, tr_cols, rf_vals, rf_cols):
    source = sources[0, 0, 0]
    rows_in, span = source.shape
    row_blocks, picks = tr_cols.shape[-2:]
    blocks = rows_in // BLOCK
    batches = BATCHES
    width = span // batches
    rows = blocks * width
    tasks = 2 * batches
    f32, bf16 = jnp.float32, jnp.bfloat16
    vmem = pl.BlockSpec(memory_space=pltpu.VMEM)
    smem = pl.BlockSpec(memory_space=pltpu.SMEM)
    hbm = pl.BlockSpec(memory_space=pl.ANY)
    dma = pltpu.SemaphoreType.DMA
    out = pl.pallas_call(
        functools.partial(kernel, (batches, width, blocks, row_blocks, picks, slabs)),
        out_shape=jax.ShapeDtypeStruct((rows_in, span), f32),
        in_specs=[vmem, hbm, hbm, smem, smem],
        out_specs=vmem,
        scratch_shapes=[
            pltpu.VMEM((tasks, PIECES, rows, BLOCK), f32),
            pltpu.VMEM((2 * KEEP, PIECES * blocks, 2 * width, BLOCK), bf16),
            pltpu.VMEM((2 * row_blocks, picks * BLOCK, 2 * BLOCK), bf16),
            pltpu.VMEM((2 * row_blocks, picks, BLOCK, BLOCK), f32),
            pltpu.VMEM((batches, rows, BLOCK), f32),
            pltpu.VMEM((blocks, span, BLOCK), f32),
            pltpu.VMEM((tasks, rows, BLOCK), f32),
            pltpu.VMEM((batches, rows, BLOCK), f32),
            pltpu.VMEM((batches, rows, BLOCK), f32),
            pltpu.VMEM((batches, rows, BLOCK), f32),
            pltpu.VMEM((3, rows, BLOCK), f32),
            pltpu.VMEM((tasks, 2, rows, BLOCK), f32),
            pltpu.VMEM((tasks, 2, rows, BLOCK), f32),
            pltpu.SMEM((2, row_blocks, picks), jnp.int32),
            dma((2 * row_blocks,)),
            dma((tasks,)),
            dma((tasks, RING - 1)),
            dma((2,)),
            dma((tasks, 2)),
            dma,
            dma((tasks,)),
            dma,
        ],
        compiler_params=pltpu.CompilerParams(
            collective_id=0,
            has_side_effects=True,
            vmem_limit_bytes=60 * 1024 * 1024,
        ),
    )(source, tr_vals[0, 0, 0], rf_vals[0, 0, 0], tr_cols[0, 0, 0][:, None], rf_cols[0, 0, 0][:, None])
    return out[None, None, None]


def solution(mesh):
    placed = (
        P("slab", "col", "row", None, None),
        P("slab", "col", "row", None, None, None, None),
        P("slab", "col", "row", None, None),
        P("slab", "col", "row", None, None, None, None),
        P("slab", "col", "row", None, None),
    )
    return jax.shard_map(
        functools.partial(shards, mesh.shape["slab"]),
        mesh=mesh,
        in_specs=placed,
        out_specs=P("slab", "col", "row", None, None),
        check_vma=False,
    )
```
